32 devices in a mesh: dp: 8 (over z, y), tensor: 4 (over x, core).
Axes of the slice: x: 2, y: 2, z: 4, core: 2. Of those that a mesh axis runs over, the one named last changes fastest.
Arguments:
- resid_in: float32 [4096, 1024], P(('dp', 'tensor')), may hold values from -6 to 6
- segment_ids: int32 [8, 512], P('dp'), may hold values from 0 to 3, never falling along the last dimension, each value on 1 to 384 neighbouring positions
- out_grad: float32 [4096, 1024], P(('dp', 'tensor')), may hold values from -6 to 6
- norm1_gain: float32 [1024], replicated, may hold values from 0.25 to 1.75
- norm1_shift: float32 [1024], replicated, may hold values from -3 to 3
- qkv_weight: bfloat16 [3, 1024, 1024], P(None, 'dp', 'tensor'), may hold values from -0.1875 to 0.1875
- qv_bias: float32 [2, 1024], P(None, 'tensor'), may hold values from -3 to 3
- proj_weight: bfloat16 [1024, 1024], P('tensor', 'dp'), may hold values from -1 to 1
- proj_bias: float32 [1024], replicated, may hold values from -3 to 3
- norm2_gain: float32 [1024], replicated, may hold values from 0.25 to 1.75
- norm2_shift: float32 [1024], replicated, may hold values from -3 to 3
- up_weight: bfloat16 [1024, 4096], P('dp', 'tensor'), may hold values from -0.1875 to 0.1875
- up_bias: float32 [4096], P('tensor'), may hold values from -3 to 3
- down_weight: bfloat16 [4096, 1024], P('tensor', 'dp'), may hold values from -0.09375 to 0.09375
- down_bias: float32 [1024], replicated, may hold values from -3 to 3
Outputs:
- resid_out: float32 [4096, 1024], P(('dp', 'tensor'))
- resid_grad: float32 [4096, 1024], P(('dp', 'tensor'))
- norm1_gain_grad: float32 [1024], replicated
- norm1_shift_grad: float32 [1024], replicated
- qkv_grad: float32 [3, 1024, 1024], P(None, 'dp', 'tensor')
- qv_bias_grad: float32 [2, 1024], P(None, 'tensor')
- proj_grad: float32 [1024, 1024], P('tensor', 'dp')
- proj_bias_grad: float32 [1024], replicated
- norm2_gain_grad: float32 [1024], replicated
- norm2_shift_grad: float32 [1024], replicated
- up_grad: float32 [1024, 4096], P('dp', 'tensor')
- up_bias_grad: float32 [4096], P('tensor')
- down_grad: float32 [4096, 1024], P('tensor', 'dp')
- down_bias_grad: float32 [1024], replicated
The draws below stay inside these ranges and needn't reach their ends.
Inputs may be any that keep to these rules, and one draw needn't show every extreme that they name: `segment_ids`: in each group the numbers never fall along the 512 tokens, every number from 0 to 3 occurs, and none covers more than 384 tokens.
All inputs are finite; a program needn't handle non-finite values.
Results may differ from the reference program's by a relative error of at most 0.013.
Values may be sent and summed in bfloat16 or wider, within the bound.
No kernel may reach another device: no remote copies, remote signals or barrier semaphores. Data moves between devices by JAX's collectives and lax.ppermute only.
A program may use at most 64 MiB of HBM per device.

```python
import math
import jax
import jax.numpy as jnp
import numpy as np
from jax import lax

D = 1024
HD = 64
FF = 4096
TOK_DEV = 512
SEQS_DEV = 4
SEQ_MAX = 384
GROUPS = 8
TOKENS = 4096


def spiked(entries, rng, source, target, blocks, factor):
    def block_of(dim):
        return (jnp.arange(entries.shape[dim]) // (entries.shape[dim] // blocks)).reshape((-1,) + (1,) * (entries.ndim - 1 - dim))

    one_side = jax.random.permutation(rng, blocks)[block_of(target)]
    other_side = (block_of(target) + blocks // 2) % blocks
    return jnp.where((block_of(source) == one_side) | (block_of(source) == other_side), factor * entries, entries)


def steps_of(own_key, extent, cuts, low, top_value):
    level, own = 1.0, jax.random.fold_in(own_key, 6)
    for position, shards_of in cuts:
        draws = jnp.exp(jax.random.uniform(jax.random.fold_in(own, position), (shards_of,), jnp.float32, low / len(cuts), top_value / len(cuts)))
        level = level * jnp.repeat(draws, extent[position] // shards_of).reshape([-1 if axis == position else 1 for axis in range(len(extent))])
    return level


def length_profile(count, total, limit, skew):
    loads = [(1 << 20) // math.isqrt(rank ** skew) + 1 for rank in range(2, count + 1)]
    rest, holding = total - limit - (count - 1), [1] * (count - 1)
    while rest > 0:
        free = [i for i in range(count - 1) if holding[i] < limit]
        mass, budget = sum([loads[i] for i in free]), rest
        for i in free:
            more = min(limit - holding[i], max(1, budget * loads[i] // mass), rest)
            holding[i] = holding[i] + more
            rest = rest - more
    return np.array([limit] + holding)


def uneven(key, count, total, bound, slope):
    if count == 2:
        one = jax.random.randint(key, (), max(1, total - bound), min(bound, total - 1) + 1)
        return jnp.stack([one, total - one])
    tallies = jnp.asarray(length_profile(count, total, bound, slope), jnp.int32)
    couples = (count - 1) // 2
    donor, receiver = tallies[1:1 + 2 * couples:2], tallies[2:2 + 2 * couples:2]
    margin = jnp.minimum(donor - 1, bound - receiver)
    moved = jax.random.randint(jax.random.fold_in(key, 1), (couples,), 0, 1 << 20) % (margin + 1)
    tallies = tallies.at[1:1 + 2 * couples:2].set(donor - moved).at[2:2 + 2 * couples:2].set(receiver + moved)
    return tallies[jax.random.permutation(jax.random.fold_in(key, 2), count)]


def scatter_about(stream_key, shape, scale, reach, cuts=(), held_as=jnp.bfloat16):
    loudness = steps_of(stream_key, shape, cuts, -0.22, 0.18) if cuts else 1.0
    array = jax.random.normal(stream_key, shape, jnp.float32) * scale * loudness
    return jnp.minimum(jnp.maximum(array, -reach), reach).astype(held_as)


def heavy_noise(key, shape, deviation, most, shards, heavy, held_as=jnp.bfloat16):
    array = deviation * jax.random.normal(key, shape, jnp.float32)
    if shards:
        array = array * steps_of(key, shape, shards, -0.22, 0.18)
    return jnp.clip(spiked(array, jax.random.fold_in(key, 3), *heavy), -most, most).astype(held_as)


def setup_inputs(seed: int = 0) -> dict:
    splits = jax.random.split(jax.random.key(seed), 16)
    resid_in = scatter_about(splits[0], (TOKENS, D), 1.0, 6.0, ((0, 32),), jnp.float32)
    segment_ids = jax.vmap(lambda own: jnp.searchsorted(jnp.cumsum(uneven(own, SEQS_DEV, TOK_DEV, SEQ_MAX, 2)), jnp.arange(TOK_DEV), side="right"))(jax.random.split(splits[1], GROUPS)).reshape((GROUPS, TOK_DEV)).astype(jnp.int32)
    out_grad = heavy_noise(splits[2], (TOKENS, D), 1.0, 6.0, ((0, 32),), (0, 1, 32, 2.75), jnp.float32)
    norm1_gain = jnp.clip(1.0 + 0.15 * jax.random.normal(splits[3], (D,), jnp.float32), 0.25, 1.75)
    norm1_shift = scatter_about(splits[4], (D,), 0.5, 3.0, (), jnp.float32)
    qkv_weight = scatter_about(splits[5], (3, D, D), D ** -0.5, 0.1875, ((1, 8), (2, 4)))
    qv_bias = scatter_about(splits[6], (2, D), 0.5, 3.0, ((1, 4),), jnp.float32)
    proj_weight = scatter_about(splits[7], (D, D), (max(D // 32, 8)) ** -0.5, 1.0, ((0, 4), (1, 8)))
    proj_bias = scatter_about(splits[8], (D,), 0.5, 3.0, (), jnp.float32)
    norm2_gain = jnp.clip(1.0 + 0.15 * jax.random.normal(splits[9], (D,), jnp.float32), 0.25, 1.75)
    norm2_shift = scatter_about(splits[10], (D,), 0.5, 3.0, (), jnp.float32)
    up_weight = scatter_about(splits[11], (D, FF), D ** -0.5, 0.1875, ((0, 8), (1, 4)))
    up_bias = scatter_about(splits[12], (FF,), 0.5, 3.0, ((0, 4),), jnp.float32)
    down_weight = scatter_about(splits[13], (FF, D), FF ** -0.5, 0.09375, ((0, 4), (1, 8)))
    down_bias = scatter_about(splits[14], (D,), 0.5, 3.0, (), jnp.float32)
    return {"resid_in": resid_in, "segment_ids": segment_ids, "out_grad": out_grad, "norm1_gain": norm1_gain, "norm1_shift": norm1_shift, "qkv_weight": qkv_weight, "qv_bias": qv_bias, "proj_weight": proj_weight, "proj_bias": proj_bias, "norm2_gain": norm2_gain, "norm2_shift": norm2_shift, "up_weight": up_weight, "up_bias": up_bias, "down_weight": down_weight, "down_bias": down_bias}


eps = 1e-05
root_coef = 0.7978845608028654

def widened(low_value):
    return lax.optimization_barrier(low_value).astype(jnp.float32)

def layer_norm(row_block, gain_vec, shift_vec):
    row_mean = lax.optimization_barrier(jnp.mean(row_block, axis=-1, keepdims=True))
    centred = row_block - row_mean
    variance = lax.optimization_barrier(jnp.mean(centred * centred, axis=-1, keepdims=True))
    return centred * lax.rsqrt(variance + eps) * gain_vec + shift_vec

def gelu_tanh(inputs):
    return 0.5 * inputs * (1.0 + jnp.tanh(root_coef * (inputs + 0.044715 * inputs * inputs * inputs)))

def segment_mask(seg_row):
    positions = jnp.arange(seg_row.shape[0])
    return (seg_row[:, None] == seg_row[None, :]) & (positions[None, :] <= positions[:, None])

def attention(query_rows, key_rows, value_rows, allowed):
    factor = query_rows.shape[-1] ** (-0.5)
    scores = jnp.einsum('qhd,khd->hqk', widened(query_rows), widened(key_rows)) * factor
    totals = lax.optimization_barrier(jnp.sum(jnp.where(allowed[None], jnp.exp(scores), 0.0), axis=-1))
    logsum = jnp.log(totals)
    attn_probs = jnp.where(allowed[None], jnp.exp(scores - logsum[..., None]), 0.0).astype(jnp.bfloat16)
    attn_mixed = jnp.einsum('hqk,khd->qhd', widened(attn_probs), widened(value_rows))
    return (attn_mixed.astype(jnp.bfloat16), logsum)

def attention_back(query_rows, key_rows, value_rows, attn_mixed, logsum, d_mixed, allowed):
    factor = query_rows.shape[-1] ** (-0.5)
    query_wide = widened(query_rows)
    key_wide = widened(key_rows)
    scores = jnp.einsum('qhd,khd->hqk', query_wide, key_wide) * factor
    attn_probs = jnp.where(allowed[None], jnp.exp(scores - logsum[..., None]), 0.0)
    d_wide = widened(d_mixed)
    d_values = jnp.einsum('hqk,qhd->khd', widened(attn_probs.astype(jnp.bfloat16)), d_wide)
    d_probs = jnp.einsum('qhd,khd->hqk', d_wide, widened(value_rows))
    row_delta = jnp.einsum('qhd,qhd->hq', d_wide, widened(attn_mixed))
    grad_scores = (attn_probs * (d_probs - row_delta[..., None]) * factor).astype(jnp.bfloat16)
    grad_wide = widened(grad_scores)
    d_query = jnp.einsum('hqk,khd->qhd', grad_wide, key_wide)
    d_keys = jnp.einsum('hqk,qhd->khd', grad_wide, query_wide)
    return (d_query, d_keys, d_values)

def group_pass(params, resid, cotangent, seg_row):
    gain_one, shift_one, w_qkv, b_qv, w_proj, b_proj, gain_two, shift_two, w_up, b_up, w_down, b_down = params
    row_total = resid.shape[0]
    split = (row_total, -1, HD)
    allowed = segment_mask(seg_row)
    normed_one = layer_norm(resid, gain_one, shift_one).astype(jnp.bfloat16)
    query_rows = (jnp.dot(normed_one, w_qkv[0], preferred_element_type=jnp.float32) + b_qv[0]).astype(jnp.bfloat16)
    key_rows = jnp.dot(normed_one, w_qkv[1], preferred_element_type=jnp.float32).astype(jnp.bfloat16)
    value_rows = (jnp.dot(normed_one, w_qkv[2], preferred_element_type=jnp.float32) + b_qv[1]).astype(jnp.bfloat16)
    attn_mixed, logsum = attention(query_rows.reshape(split), key_rows.reshape(split), value_rows.reshape(split), allowed)
    mixed_flat = attn_mixed.reshape(row_total, -1)
    middle = resid + jnp.dot(mixed_flat, w_proj, preferred_element_type=jnp.float32) + b_proj
    normed_two = layer_norm(middle, gain_two, shift_two).astype(jnp.bfloat16)
    upper = jnp.dot(normed_two, w_up, preferred_element_type=jnp.float32) + b_up
    hidden = gelu_tanh(upper).astype(jnp.bfloat16)
    resid_out = middle + jnp.dot(hidden, w_down, preferred_element_type=jnp.float32) + b_down
    cot_b = cotangent.astype(jnp.bfloat16)
    g_down = jnp.dot(hidden.T, cot_b, preferred_element_type=jnp.float32)
    d_hidden = jnp.dot(cot_b, w_down.T, preferred_element_type=jnp.float32)
    d_upper = jax.vjp(gelu_tanh, upper)[1](d_hidden)[0]
    d_upper_b = d_upper.astype(jnp.bfloat16)
    g_up = jnp.dot(normed_two.T, d_upper_b, preferred_element_type=jnp.float32)
    g_upbias = lax.optimization_barrier(jnp.sum(d_upper, axis=0))
    d_two = jnp.dot(d_upper_b, w_up.T, preferred_element_type=jnp.float32)
    d_mid_norm, g_gain_two, g_shift_two = jax.vjp(layer_norm, middle, gain_two, shift_two)[1](d_two)
    d_middle = cotangent + d_mid_norm
    d_middle_b = d_middle.astype(jnp.bfloat16)
    g_proj = jnp.dot(mixed_flat.T, d_middle_b, preferred_element_type=jnp.float32)
    d_mixed = jnp.dot(d_middle_b, w_proj.T, preferred_element_type=jnp.float32).astype(jnp.bfloat16)
    d_query, d_keys, d_values = attention_back(query_rows.reshape(split), key_rows.reshape(split), value_rows.reshape(split), attn_mixed, logsum, d_mixed.reshape(split), allowed)
    d_query = d_query.reshape(row_total, -1)
    d_keys = d_keys.reshape(row_total, -1)
    d_values = d_values.reshape(row_total, -1)
    g_qvbias = jnp.stack([lax.optimization_barrier(jnp.sum(d_query, axis=0)), lax.optimization_barrier(jnp.sum(d_values, axis=0))])
    dq_b = d_query.astype(jnp.bfloat16)
    dk_b = d_keys.astype(jnp.bfloat16)
    dv_b = d_values.astype(jnp.bfloat16)
    g_qkv = jnp.stack([jnp.dot(normed_one.T, dq_b, preferred_element_type=jnp.float32), jnp.dot(normed_one.T, dk_b, preferred_element_type=jnp.float32), jnp.dot(normed_one.T, dv_b, preferred_element_type=jnp.float32)])
    d_one = jnp.dot(dq_b, w_qkv[0].T, preferred_element_type=jnp.float32) + jnp.dot(dk_b, w_qkv[1].T, preferred_element_type=jnp.float32) + jnp.dot(dv_b, w_qkv[2].T, preferred_element_type=jnp.float32)
    d_in_norm, g_gain_one, g_shift_one = jax.vjp(layer_norm, resid, gain_one, shift_one)[1](d_one)
    resid_grad = d_middle + d_in_norm
    grads = (g_gain_one, g_shift_one, g_qkv, g_qvbias, g_proj, lax.optimization_barrier(jnp.sum(d_middle, axis=0)), g_gain_two, g_shift_two, g_up, g_upbias, g_down, lax.optimization_barrier(jnp.sum(cotangent, axis=0)))
    return (resid_out, resid_grad, grads)

def reference(resid_in, segment_ids, out_grad, norm1_gain, norm1_shift, qkv_weight, qv_bias, proj_weight, proj_bias, norm2_gain, norm2_shift, up_weight, up_bias, down_weight, down_bias):
    params = (norm1_gain, norm1_shift, qkv_weight, qv_bias, proj_weight, proj_bias, norm2_gain, norm2_shift, up_weight, up_bias, down_weight, down_bias)
    zero_grads = jax.tree.map(lambda param: jnp.zeros(param.shape, jnp.float32), params)

    def group_step(carried, inputs):
        resid, cotangent, seg_row = inputs
        resid_out, resid_grad, grads = group_pass(params, resid, cotangent, seg_row)
        carried = jax.tree.map(lambda left, right: left + right, carried, grads)
        return (carried, (resid_out, resid_grad))
    sums, (outs_all, grads_all) = lax.scan(group_step, zero_grads, (resid_in.reshape(GROUPS, TOK_DEV, D), out_grad.reshape(GROUPS, TOK_DEV, D), segment_ids))
    return (outs_all.reshape(TOKENS, D), grads_all.reshape(TOKENS, D), sums[0], sums[1], sums[2], sums[3], sums[4], sums[5], sums[6], sums[7], sums[8], sums[9], sums[10], sums[11])
```

```python
import jax
import jax.numpy as jnp
from jax import lax
from jax.experimental import pallas as pl
from jax.experimental.pallas import tpu as pltpu
from jax.sharding import PartitionSpec as P

HD = 64
BF = jnp.bfloat16
F32 = jnp.float32

eps = 1e-05
root_coef = 0.7978845608028654


def layer_norm(row_block, gain_vec, shift_vec):
    row_mean = jnp.mean(row_block, axis=-1, keepdims=True)
    centred = row_block - row_mean
    variance = jnp.mean(centred * centred, axis=-1, keepdims=True)
    return centred * lax.rsqrt(variance + eps) * gain_vec + shift_vec


def gelu_tanh(inputs):
    return (
        0.5 * inputs * (1.0 + jnp.tanh(root_coef * (inputs + 0.044715 * inputs * inputs * inputs)))
    )


def attention(query_rows, key_rows, value_rows, allowed):
    factor = query_rows.shape[-1] ** (-0.5)
    scores = (
        jnp.einsum("qhd,khd->hqk", query_rows, key_rows, preferred_element_type=F32) * factor
    )
    totals = jnp.sum(jnp.where(allowed[None], jnp.exp(scores), 0.0), axis=-1)
    logsum = jnp.log(totals)
    attn_probs = jnp.where(allowed[None], jnp.exp(scores - logsum[..., None]), 0.0).astype(BF)
    attn_mixed = jnp.einsum("hqk,khd->qhd", attn_probs, value_rows, preferred_element_type=F32)
    return (attn_mixed.astype(BF), logsum)


def attention_back(query_rows, key_rows, value_rows, attn_mixed, logsum, d_mixed, allowed):
    factor = query_rows.shape[-1] ** (-0.5)
    scores = (
        jnp.einsum("qhd,khd->hqk", query_rows, key_rows, preferred_element_type=F32) * factor
    )
    attn_probs = jnp.where(allowed[None], jnp.exp(scores - logsum[..., None]), 0.0)
    d_values = jnp.einsum("hqk,qhd->khd", attn_probs.astype(BF), d_mixed, preferred_element_type=F32)
    d_probs = jnp.einsum("qhd,khd->hqk", d_mixed, value_rows, preferred_element_type=F32)
    row_delta = jnp.einsum("qhd,qhd->hq", d_mixed, attn_mixed, preferred_element_type=F32)
    grad_scores = (attn_probs * (d_probs - row_delta[..., None]) * factor).astype(BF)
    d_query = jnp.einsum("hqk,khd->qhd", grad_scores, key_rows, preferred_element_type=F32)
    d_keys = jnp.einsum("hqk,qhd->khd", grad_scores, query_rows, preferred_element_type=F32)
    return (d_query, d_keys, d_values)


class Axis:
    def __init__(self, name, size, most):
        self.name = name
        self.size = size
        rest, self.digits = size, []
        while rest > 1:
            step = next((s for s in range(most, 1, -1) if rest % s == 0), rest)
            self.digits.append(step)
            rest //= step
        self.strides = []
        rest = size
        for step in self.digits:
            rest //= step
            self.strides.append(rest)

    def send(self, x, pos, k):
        step, stride = self.digits[pos], self.strides[pos]
        pairs = []
        for dst in range(self.size):
            digit = dst // stride % step
            pairs.append((dst + ((digit + k) % step - digit) * stride, dst))
        return lax.ppermute(x, self.name, pairs)

    def order(self):
        own = lax.axis_index(self.name)
        blocks = [jnp.int32(0)]
        for step, stride in zip(self.digits, self.strides):
            digit = own // stride % step
            blocks = [b + (digit + k) % step * stride for k in range(step) for b in blocks]
        return jnp.stack(blocks).astype(jnp.int32)

    def gather(self, x, dim):
        for pos, step in enumerate(self.digits):
            x = jnp.concatenate([x] + [self.send(x, pos, k) for k in range(1, step)], axis=dim)
        return x

    def reduce(self, x, dim):
        for pos in reversed(range(len(self.digits))):
            step = self.digits[pos]
            width = x.shape[dim] // step
            part = lambda k: lax.slice_in_dim(x, k * width, (k + 1) * width, axis=dim)
            got = [self.send(part(k).astype(BF), pos, step - k) for k in range(1, step)]
            total = part(0)
            for piece in got:
                total = total + piece.astype(F32)
            x = total
        return x

    def total(self, x):
        stride = 1
        while stride < self.size:
            pairs = [(i, i ^ stride) for i in range(self.size)]
            x = x + lax.ppermute(x, self.name, pairs)
            stride *= 2
        return x


def copy_kernel(order_ref, *refs):
    half = len(refs) // 2
    for src, dst in zip(refs[:half], refs[half:]):
        dst[...] = src[...]


def reorder(arrays, order, inverse=False):
    count = order.shape[0]
    width = arrays[0].shape[1] // count
    if width % 128:
        if inverse:
            steps = jnp.arange(count)
            order = jnp.sum(jnp.where(order[None] == steps[:, None], steps[None], 0), axis=1)
        columns = (order[:, None] * width + jnp.arange(width)[None]).reshape(-1)
        return [jnp.take(a, columns, axis=1) for a in arrays]
    moved = lambda j, order_ref: (0, order_ref[j])
    plain = lambda j, order_ref: (0, j)
    src, dst = (plain, moved) if inverse else (moved, plain)
    return pl.pallas_call(
        copy_kernel,
        grid_spec=pltpu.PrefetchScalarGridSpec(
            num_scalar_prefetch=1,
            grid=(count,),
            in_specs=[pl.BlockSpec((a.shape[0], width), src) for a in arrays],
            out_specs=[pl.BlockSpec((a.shape[0], width), dst) for a in arrays],
        ),
        out_shape=[jax.ShapeDtypeStruct(a.shape, a.dtype) for a in arrays],
    )(order, *arrays)


def make_per_device(mesh):
    dp = Axis("dp", mesh.shape["dp"], 4)
    tp = Axis("tensor", mesh.shape["tensor"], 2)

    def per_device(
        resid_in,
        segment_ids,
        out_grad,
        norm1_gain,
        norm1_shift,
        qkv_weight,
        qv_bias,
        proj_weight,
        proj_bias,
        norm2_gain,
        norm2_shift,
        up_weight,
        up_bias,
        down_weight,
        down_bias,
    ):
        width = resid_in.shape[1]
        d_order = dp.order()
        vectors = jnp.stack(
            [norm1_gain, norm1_shift, norm2_gain, norm2_shift, proj_bias, down_bias]
        )
        resid_in, out_grad, vectors = reorder([resid_in, out_grad, vectors], d_order)
        norm1_gain, norm1_shift, norm2_gain, norm2_shift, proj_bias, down_bias = vectors

        normed_one = layer_norm(resid_in, norm1_gain, norm1_shift).astype(BF)
        rows_one = tp.gather(normed_one, 0)
        qkv_full = dp.gather(qkv_weight, 1)
        proj_full = dp.gather(proj_weight, 1)
        up_full = dp.gather(up_weight, 0)
        down_full = dp.gather(down_weight, 1)
        cot_all = tp.gather(out_grad.astype(BF), 0)

        group_rows = rows_one.shape[0]
        rows_dev = resid_in.shape[0]
        t_order = tp.order()
        positions = (t_order[:, None] * rows_dev + jnp.arange(rows_dev)[None]).reshape(-1)
        seg = jnp.concatenate(
            [
                lax.dynamic_slice_in_dim(segment_ids[0], t_order[k] * rows_dev, rows_dev)
                for k in range(tp.size)
            ]
        )
        allowed = (seg[:, None] == seg[None, :]) & (positions[None, :] <= positions[:, None])

        split = (group_rows, -1, HD)
        query_rows = (
            jnp.dot(rows_one, qkv_full[0], preferred_element_type=F32) + qv_bias[0]
        ).astype(BF)
        key_rows = jnp.dot(rows_one, qkv_full[1], preferred_element_type=F32).astype(BF)
        value_rows = (
            jnp.dot(rows_one, qkv_full[2], preferred_element_type=F32) + qv_bias[1]
        ).astype(BF)
        attn_mixed, logsum = attention(
            query_rows.reshape(split), key_rows.reshape(split), value_rows.reshape(split), allowed
        )
        mixed_flat = attn_mixed.reshape(group_rows, -1)
        attn_rows = tp.reduce(jnp.dot(mixed_flat, proj_full, preferred_element_type=F32), 0)
        middle = resid_in + attn_rows + proj_bias
        normed_two = layer_norm(middle, norm2_gain, norm2_shift).astype(BF)
        rows_two = tp.gather(normed_two, 0)
        upper = jnp.dot(rows_two, up_full, preferred_element_type=F32) + up_bias
        hidden = gelu_tanh(upper).astype(BF)
        g_down = jnp.einsum("tf,td->fd", hidden, cot_all, preferred_element_type=F32)
        down_grad = dp.reduce(g_down, 1)
        d_hidden = jnp.einsum("td,fd->tf", cot_all, down_full, preferred_element_type=F32)
        d_upper = jax.vjp(gelu_tanh, upper)[1](d_hidden)[0]
        d_upper_b = d_upper.astype(BF)
        g_up = jnp.einsum("td,tf->df", rows_two, d_upper_b, preferred_element_type=F32)
        up_grad = dp.reduce(g_up, 0)
        g_upbias = jnp.sum(d_upper, axis=0)
        d_two = tp.reduce(
            jnp.einsum("tf,df->td", d_upper_b, up_full, preferred_element_type=F32), 0
        )
        mlp_rows = tp.reduce(jnp.dot(hidden, down_full, preferred_element_type=F32), 0)
        resid_out = middle + mlp_rows + down_bias
        d_mid_norm, g_gain_two, g_shift_two = jax.vjp(layer_norm, middle, norm2_gain, norm2_shift)[
            1
        ](d_two)
        d_middle = out_grad + d_mid_norm
        middle_all = tp.gather(d_middle.astype(BF), 0)
        g_proj = jnp.einsum("tc,td->cd", mixed_flat, middle_all, preferred_element_type=F32)
        proj_grad = dp.reduce(g_proj, 1)
        d_mixed = jnp.einsum("td,cd->tc", middle_all, proj_full, preferred_element_type=F32).astype(
            BF
        )
        d_query, d_keys, d_values = attention_back(
            query_rows.reshape(split),
            key_rows.reshape(split),
            value_rows.reshape(split),
            attn_mixed,
            logsum,
            d_mixed.reshape(split),
            allowed,
        )
        d_query = d_query.reshape(group_rows, -1)
        d_keys = d_keys.reshape(group_rows, -1)
        d_values = d_values.reshape(group_rows, -1)
        g_qvbias = jnp.stack([jnp.sum(d_query, axis=0), jnp.sum(d_values, axis=0)])
        dq_b = d_query.astype(BF)
        dk_b = d_keys.astype(BF)
        dv_b = d_values.astype(BF)
        g_qkv = jnp.stack(
            [
                jnp.einsum("td,tc->dc", rows_one, dq_b, preferred_element_type=F32),
                jnp.einsum("td,tc->dc", rows_one, dk_b, preferred_element_type=F32),
                jnp.einsum("td,tc->dc", rows_one, dv_b, preferred_element_type=F32),
            ]
        )
        qkv_grad = dp.reduce(g_qkv, 1)
        d_one = tp.reduce(
            jnp.einsum("tc,dc->td", dq_b, qkv_full[0], preferred_element_type=F32)
            + jnp.einsum("tc,dc->td", dk_b, qkv_full[1], preferred_element_type=F32)
            + jnp.einsum("tc,dc->td", dv_b, qkv_full[2], preferred_element_type=F32),
            0,
        )
        d_in_norm, g_gain_one, g_shift_one = jax.vjp(layer_norm, resid_in, norm1_gain, norm1_shift)[
            1
        ](d_one)
        resid_grad = d_middle + d_in_norm
        sums = jnp.stack(
            [
                g_gain_one,
                g_shift_one,
                jnp.sum(d_middle, axis=0),
                g_gain_two,
                g_shift_two,
                jnp.sum(out_grad, axis=0),
            ]
        )
        resid_out, resid_grad, sums = reorder([resid_out, resid_grad, sums], d_order, True)
        sums = tp.total(sums)
        packed = jnp.concatenate([sums.reshape(-1), g_qvbias.reshape(-1), g_upbias])
        packed = dp.total(packed)
        cut = sums.size
        vec = packed[:cut].reshape(sums.shape)
        qv_bias_grad = packed[cut : cut + g_qvbias.size].reshape(g_qvbias.shape)
        up_bias_grad = packed[cut + g_qvbias.size :]
        return (
            resid_out,
            resid_grad,
            vec[0],
            vec[1],
            qkv_grad,
            qv_bias_grad,
            proj_grad,
            vec[2],
            vec[3],
            vec[4],
            up_grad,
            up_bias_grad,
            down_grad,
            vec[5],
        )

    return per_device


def solution(mesh):
    rows = P(("dp", "tensor"), None)
    qkv = P(None, "dp", "tensor")
    in_specs = (
        rows,
        P("dp", None),
        rows,
        P(),
        P(),
        qkv,
        P(None, "tensor"),
        P("tensor", "dp"),
        P(),
        P(),
        P(),
        P("dp", "tensor"),
        P("tensor"),
        P("tensor", "dp"),
        P(),
    )
    out_specs = (
        rows,
        rows,
        P(),
        P(),
        qkv,
        P(None, "tensor"),
        P("tensor", "dp"),
        P(),
        P(),
        P(),
        P("dp", "tensor"),
        P("tensor"),
        P("tensor", "dp"),
        P(),
    )
    return jax.shard_map(
        make_per_device(mesh), mesh=mesh, in_specs=in_specs, out_specs=out_specs, check_vma=False
    )
```

```python
import functools

import jax
import jax.numpy as jnp
from jax import lax
from jax.experimental import pallas as pl
from jax.experimental.pallas import tpu as pltpu
from jax.sharding import PartitionSpec as P

HD = 64
LANES = 128
BF = jnp.bfloat16
F32 = jnp.float32

eps = 1e-05
root_coef = 0.7978845608028654
cube_coef = 0.044715


class Axis:
    def __init__(self, name, size, most):
        self.name = name
        self.size = size
        rest, self.digits = size, []
        while rest > 1:
            step = next((s for s in range(most, 1, -1) if rest % s == 0), rest)
            self.digits.append(step)
            rest //= step
        self.strides = []
        rest = size
        for step in self.digits:
            rest //= step
            self.strides.append(rest)

    def send(self, x, pos, k):
        step, stride = self.digits[pos], self.strides[pos]
        pairs = []
        for dst in range(self.size):
            digit = dst // stride % step
            pairs.append((dst + ((digit + k) % step - digit) * stride, dst))
        return lax.ppermute(x, self.name, pairs)

    def order(self):
        own = lax.axis_index(self.name)
        blocks = [jnp.int32(0)]
        for step, stride in zip(self.digits, self.strides):
            digit = own // stride % step
            blocks = [b + (digit + k) % step * stride for k in range(step) for b in blocks]
        return jnp.stack(blocks).astype(jnp.int32)

    def gather(self, x, dim, label):
        pieces = [x]
        for pos, step in enumerate(self.digits):
            if pos > 1:
                pieces = [jnp.concatenate(pieces, axis=dim)]
            new = list(pieces)
            for k in range(1, step):
                for number, piece in enumerate(pieces):
                    kind = "own" if number == 0 else "rest"
                    with jax.named_scope(f"{label}_{pos}_{kind}"):
                        new.append(self.send(piece, pos, k))
            pieces = new
        return jnp.concatenate(pieces, axis=dim)

    def exchange(self, sends, pos, label):
        got = []
        for k, piece in enumerate(sends, 1):
            with jax.named_scope(f"{label}_{pos}"):
                got.append(self.send(piece, pos, self.digits[pos] - k))
        return got

    def scatter(self, keep, sends, dim, label, pos):
        got = self.exchange(sends, pos, label)
        while pos > 0:
            pos -= 1
            total = keep
            for piece in got:
                total = total + piece.astype(F32)
            width = total.shape[dim] // self.digits[pos]
            parts = [
                lax.slice_in_dim(total, k * width, (k + 1) * width, axis=dim)
                for k in range(self.digits[pos])
            ]
            keep = parts[0]
            got = self.exchange([p.astype(BF) for p in parts[1:]], pos, label)
        return [keep] + got

    def total(self, x, label):
        stride = 1
        while stride < self.size:
            pairs = [(i, i ^ stride) for i in range(self.size)]
            with jax.named_scope(f"{label}_{stride}"):
                x = x + lax.ppermute(x, self.name, pairs)
            stride *= 2
        return x


def add_up(parts):
    total = parts[0].astype(F32)
    for piece in parts[1:]:
        total = total + piece.astype(F32)
    return total


def dot_nn(a, b):
    return lax.dot_general(a, b, (((1,), (0,)), ((), ())), preferred_element_type=F32)


def dot_nt(a, b):
    return lax.dot_general(a, b, (((1,), (1,)), ((), ())), preferred_element_type=F32)


def dot_tn(a, b):
    return lax.dot_general(a, b, (((0,), (0,)), ((), ())), preferred_element_type=F32)


def run(name, body, outs, args, scratch=(), smem=0, flops=0):
    out_shape = [jax.ShapeDtypeStruct(shape, dtype) for shape, dtype in outs]
    moved = sum(a.size * a.dtype.itemsize for a in list(args) + out_shape)
    specs = [
        pl.BlockSpec(memory_space=pltpu.SMEM if i < smem else pltpu.VMEM) for i in range(len(args))
    ]
    with jax.named_scope(name):
        return pl.pallas_call(
            body,
            in_specs=specs,
            out_specs=[pl.BlockSpec(memory_space=pltpu.VMEM) for _ in outs],
            out_shape=out_shape,
            scratch_shapes=list(scratch),
            cost_estimate=pl.CostEstimate(flops=flops, transcendentals=0, bytes_accessed=moved),
            name=name,
        )(*args)


class Columns:
    def __init__(self, order, width):
        self.order = order
        self.count = order.shape[0]
        self.width = width
        self.block = width // self.count
        self.aligned = self.block % LANES == 0

    def table(self):
        return self.order if self.aligned else jnp.zeros((1,), jnp.int32)

    def spots(self, order_ref):
        if not self.aligned:
            return [(slice(0, self.width), slice(0, self.width))]
        return [
            (
                slice(j * self.block, (j + 1) * self.block),
                pl.ds(pl.multiple_of(order_ref[j] * self.block, LANES), self.block),
            )
            for j in range(self.count)
        ]

    def columns(self, order):
        return (order[:, None] * self.block + jnp.arange(self.block)[None]).reshape(-1)

    def relative(self, x):
        return x if self.aligned else jnp.take(x, self.columns(self.order), axis=1)

    def whole(self, x):
        if self.aligned:
            return x
        steps = jnp.arange(self.count)
        inverse = jnp.sum(jnp.where(self.order[None] == steps[:, None], steps[None], 0), axis=1)
        return jnp.take(x, self.columns(inverse), axis=1)


def centre(rows):
    c = rows - jnp.mean(rows, axis=-1, keepdims=True)
    return c, lax.rsqrt(jnp.mean(c * c, axis=-1, keepdims=True) + eps)


def entry(cols, resid, out_grad, gain, shift):
    def body(order_ref, x_ref, g_ref, gain_ref, shift_ref, n_ref, c_ref, sum_ref, hold):
        c, scale = centre(x_ref[...])
        hold[...] = c * scale * gain_ref[...] + shift_ref[...]
        for rel, own in cols.spots(order_ref):
            n_ref[:, rel] = hold[:, own].astype(BF)
            c_ref[:, rel] = g_ref[:, own].astype(BF)
        sum_ref[...] = jnp.sum(g_ref[...], axis=0, keepdims=True)

    shape = resid.shape
    normed, cot, total = run(
        "entry",
        body,
        [(shape, BF), (shape, BF), ((1, shape[1]), F32)],
        [cols.table(), resid, out_grad, gain, shift],
        [pltpu.VMEM(shape, F32)],
        smem=1,
    )
    return cols.relative(normed), cols.relative(cot), total


def second_norm(cols, resid, parts, bias, gain, shift):
    parts = [cols.whole(p) for p in parts]

    def body(order_ref, x_ref, bias_ref, gain_ref, shift_ref, *refs):
        part_refs, (mid_ref, n_ref, hold) = refs[: len(parts)], refs[len(parts) :]
        for rel, own in cols.spots(order_ref):
            hold[:, own] = add_up([p[:, rel] for p in part_refs])
        middle = x_ref[...] + hold[...] + bias_ref[...]
        mid_ref[...] = middle
        c, scale = centre(middle)
        hold[...] = c * scale * gain_ref[...] + shift_ref[...]
        for rel, own in cols.spots(order_ref):
            n_ref[:, rel] = hold[:, own].astype(BF)

    shape = resid.shape
    middle, normed = run(
        "second_norm",
        body,
        [(shape, F32), (shape, BF)],
        [cols.table(), resid, bias, gain, shift, *parts],
        [pltpu.VMEM(shape, F32)],
        smem=1,
    )
    return middle, cols.relative(normed)


def last_add(cols, middle, parts, bias):
    parts = [cols.whole(p) for p in parts]

    def body(order_ref, x_ref, bias_ref, *refs):
        part_refs, out_ref = refs[:-1], refs[-1]
        for rel, own in cols.spots(order_ref):
            out_ref[:, own] = (
                x_ref[:, own] + add_up([p[:, rel] for p in part_refs]) + bias_ref[:, own]
            )

    return run(
        "last_add",
        body,
        [(middle.shape, F32)],
        [cols.table(), middle, bias, *parts],
        smem=1,
    )[0]


def norm_back(name, cols, rows, parts, gain, upstream, need_rel):
    parts = [cols.whole(p) for p in parts]

    def body(order_ref, x_ref, gain_ref, up_ref, *refs):
        part_refs, (out_ref, ggain_ref, gshift_ref, *more) = refs[: len(parts)], refs[len(parts) :]
        hold = more[-1]
        for rel, own in cols.spots(order_ref):
            hold[:, own] = add_up([p[:, rel] for p in part_refs])
        d = hold[...]
        c, scale = centre(x_ref[...])
        xhat = c * scale
        ggain_ref[...] = jnp.sum(d * xhat, axis=0, keepdims=True)
        gshift_ref[...] = jnp.sum(d, axis=0, keepdims=True)
        dx = d * gain_ref[...]
        dx = dx - jnp.mean(dx, axis=-1, keepdims=True) - xhat * jnp.mean(
            dx * xhat, axis=-1, keepdims=True
        )
        out = up_ref[...] + scale * dx
        out_ref[...] = out
        if need_rel:
            more[1][...] = jnp.sum(out, axis=0, keepdims=True)
            for rel, own in cols.spots(order_ref):
                more[0][:, rel] = out_ref[:, own].astype(BF)

    shape = rows.shape
    vec = ((1, shape[1]), F32)
    outs = [(shape, F32), vec, vec] + ([(shape, BF), vec] if need_rel else [])
    return run(
        name,
        body,
        outs,
        [cols.table(), rows, gain, upstream, *parts],
        [pltpu.VMEM(shape, F32)],
        smem=1,
    )


def lane_mask(e, value, dtype):
    lanes = lax.broadcasted_iota(jnp.int32, (1, LANES), 1)
    return jnp.where(lanes // HD == e, value, 0.0).astype(dtype)


def mask_bias(place, row0, count):
    seg_row, pos_row, seg_col, pos_col = place
    rows = pl.ds(row0, count)
    ok = (seg_col[rows, :] == seg_row[...]) & (pos_row[...] <= pos_col[rows, :])
    return jnp.where(ok, 0.0, -jnp.inf)


def attention(rows, weight, bias, place, proj, outer):
    total_rows, width = rows.shape
    cols = weight.shape[2]
    step = min(LANES, total_rows)
    cut = total_rows // outer

    def body(rows_ref, w_ref, b_ref, sr, pr, sc, pc, proj_ref, q_ref, k_ref, v_ref, m_ref, l_ref, keep, *sends):
        x = rows_ref[...]
        q_ref[...] = (dot_nn(x, w_ref[0]) + b_ref[0:1, :]).astype(BF)
        k_ref[...] = dot_nn(x, w_ref[1]).astype(BF)
        v_ref[...] = (dot_nn(x, w_ref[2]) + b_ref[1:2, :]).astype(BF)
        for row0 in range(0, total_rows, step):
            at = pl.ds(row0, step)
            floor = mask_bias((sr, pr, sc, pc), row0, step)
            logs = jnp.zeros((step, LANES), F32)
            which = lax.broadcasted_iota(jnp.int32, (1, LANES), 1)
            for first in range(0, cols, LANES):
                block = slice(first, first + LANES)
                mixed = jnp.zeros((step, LANES), F32)
                for e in range(LANES // HD):
                    own = q_ref[at, block] * lane_mask(e, HD**-0.5, BF)
                    s = dot_nt(own, k_ref[:, block]) + floor
                    logsum = jnp.log(jnp.sum(jnp.exp(s), axis=1, keepdims=True))
                    probs = jnp.exp(s - logsum).astype(BF)
                    mixed = mixed + dot_nn(probs, v_ref[:, block] * lane_mask(e, 1.0, BF))
                    logs = jnp.where(which == first // HD + e, logsum, logs)
                m_ref[at, block] = mixed.astype(BF)
            l_ref[at, :] = logs
        for k in range(outer):
            part = dot_nn(m_ref[k * cut : (k + 1) * cut, :], proj_ref[...])
            if k == 0:
                keep[...] = part
            else:
                sends[k - 1][...] = part.astype(BF)

    flat = ((total_rows, cols), BF)
    outs = [flat] * 4 + [((total_rows, LANES), F32), ((cut, width), F32)]
    outs += [((cut, width), BF)] * (outer - 1)
    got = run(
        "attention",
        body,
        outs,
        [rows, weight, bias, *place, proj],
        flops=2 * total_rows * width * cols * 4 + 4 * total_rows * total_rows * cols * 2,
    )
    return got[:5], got[5], got[6:]


def attention_back(d_rows, proj, saved, place, weight, outer):
    query, key, value, mixed, logs = saved
    total_rows, cols = query.shape
    width = d_rows.shape[1]
    step = min(LANES, total_rows)
    cut = total_rows // outer

    def body(d_ref, proj_ref, q_ref, k_ref, v_ref, m_ref, l_ref, sr, pr, sc, pc, w_ref, dqkv, bias_ref, keep, *rest):
        sends, (dm, dq, dk, dv) = rest[:-4], rest[-4:]
        dm[...] = dot_nt(d_ref[...], proj_ref[...]).astype(BF)
        for row0 in range(0, total_rows, step):
            at = pl.ds(row0, step)
            floor = mask_bias((sr, pr, sc, pc), row0, step)
            for first in range(0, cols, LANES):
                block = slice(first, first + LANES)
                acc_q = jnp.zeros((step, LANES), F32)
                for e in range(LANES // HD):
                    scaled = lane_mask(e, HD**-0.5, BF)
                    own = q_ref[at, block] * scaled
                    s = dot_nt(own, k_ref[:, block]) + floor
                    head = first // HD + e
                    p = jnp.exp(s - l_ref[at, head : head + 1])
                    d_own = dm[at, block] * lane_mask(e, 1.0, BF)
                    delta = jnp.sum(
                        d_own.astype(F32) * m_ref[at, block].astype(F32), axis=1, keepdims=True
                    )
                    gs = (p * (dot_nt(d_own, v_ref[:, block]) - delta)).astype(BF)
                    acc_q = acc_q + dot_nn(gs, k_ref[:, block] * scaled)
                    add_k = dot_tn(gs, own)
                    add_v = dot_tn(p.astype(BF), d_own)
                    if row0 == 0 and e == 0:
                        dk[:, block] = add_k
                        dv[:, block] = add_v
                    else:
                        dk[:, block] += add_k
                        dv[:, block] += add_v
                dq[at, block] = acc_q
        for i, grad in enumerate((dq, dk, dv)):
            dqkv[:, i * cols : (i + 1) * cols] = grad[...].astype(BF)
        bias_ref[0:1, :] = jnp.sum(dq[...], axis=0, keepdims=True)
        bias_ref[1:2, :] = jnp.sum(dv[...], axis=0, keepdims=True)
        for k in range(outer):
            at = slice(k * cut, (k + 1) * cut)
            part = dot_nt(dqkv[at, 0:cols], w_ref[0])
            for i in (1, 2):
                part = part + dot_nt(dqkv[at, i * cols : (i + 1) * cols], w_ref[i])
            if k == 0:
                keep[...] = part
            else:
                sends[k - 1][...] = part.astype(BF)

    outs = [((total_rows, 3 * cols), BF), ((2, cols), F32), ((cut, width), F32)]
    outs += [((cut, width), BF)] * (outer - 1)
    grad = pltpu.VMEM((total_rows, cols), F32)
    got = run(
        "attention_back",
        body,
        outs,
        [d_rows, proj, *saved, *place, weight],
        [pltpu.VMEM((total_rows, cols), BF), grad, grad, grad],
        flops=2 * total_rows * width * cols * 4 + 10 * total_rows * total_rows * cols * 2,
    )
    return got[0], got[1], got[2], got[3:]


def feed_up(rows, weight, bias):
    total_rows = rows.shape[0]
    hidden_cols = weight.shape[1]
    step = min(LANES, total_rows)

    def body(x_ref, w_ref, b_ref, h_ref, slope_ref):
        for row0 in range(0, total_rows, step):
            at = pl.ds(row0, step)
            u = dot_nn(x_ref[at, :], w_ref[...]) + b_ref[...]
            t = jnp.tanh(root_coef * (u + cube_coef * u * u * u))
            h_ref[at, :] = (0.5 * u * (1.0 + t)).astype(BF)
            inner = root_coef * (1.0 + 3.0 * cube_coef * u * u)
            slope_ref[at, :] = 0.5 * (1.0 + t) + 0.5 * u * (1.0 - t * t) * inner

    flat = (total_rows, hidden_cols)
    return run(
        "feed_up",
        body,
        [(flat, BF), (flat, F32)],
        [rows, weight, bias],
        flops=2 * rows.size * hidden_cols,
    )


def feed_back(cot, down, slope, up, outer):
    total_rows, width = cot.shape
    hidden_cols = slope.shape[1]
    step = min(LANES, total_rows // outer)
    cut = total_rows // outer

    def body(c_ref, down_ref, s_ref, up_ref, d_ref, bias_ref, keep, *sends):
        sums = jnp.zeros((1, hidden_cols), F32)
        for row0 in range(0, total_rows, step):
            at = pl.ds(row0, step)
            d = dot_nt(c_ref[at, :], down_ref[...]) * s_ref[at, :]
            sums = sums + jnp.sum(d, axis=0, keepdims=True)
            low = d.astype(BF)
            d_ref[at, :] = low
            part = dot_nt(low, up_ref[...])
            k, offset = divmod(row0, cut)
            if k == 0:
                keep[offset : offset + step, :] = part
            else:
                sends[k - 1][offset : offset + step, :] = part.astype(BF)
        bias_ref[...] = sums

    outs = [((total_rows, hidden_cols), BF), ((1, hidden_cols), F32), ((cut, width), F32)]
    outs += [((cut, width), BF)] * (outer - 1)
    got = run(
        "feed_back",
        body,
        outs,
        [cot, down, slope, up],
        flops=4 * cot.size * hidden_cols,
    )
    return got[0], got[1], got[2], got[3:]


def feed_down(hidden, weight, outer):
    total_rows = hidden.shape[0]
    width = weight.shape[1]
    cut = total_rows // outer

    def body(h_ref, w_ref, keep, *sends):
        for k in range(outer):
            part = dot_nn(h_ref[k * cut : (k + 1) * cut, :], w_ref[...])
            if k == 0:
                keep[...] = part
            else:
                sends[k - 1][...] = part.astype(BF)

    outs = [((cut, width), F32)] + [((cut, width), BF)] * (outer - 1)
    got = run("feed_down", body, outs, [hidden, weight], flops=2 * hidden.size * width)
    return got[0], got[1:]


def weight_grad(name, axis, left, right, side):
    pos = len(axis.digits) - 1
    step = axis.digits[pos]
    wide = (left, right)[side].shape[1] // step
    shape = (wide, right.shape[1]) if side == 0 else (left.shape[1], wide)
    flops = 2 * left.shape[0] * shape[0] * shape[1]

    def block(left_ref, right_ref, k):
        at = slice(k * wide, (k + 1) * wide)
        if side == 0:
            return dot_tn(left_ref[:, at], right_ref[...])
        return dot_tn(left_ref[...], right_ref[:, at])

    def first(left_ref, right_ref, *sends):
        for k, send in enumerate(sends, 1):
            send[...] = block(left_ref, right_ref, k).astype(BF)

    sends = run(
        name + "_send", first, [(shape, BF)] * (step - 1), [left, right], flops=flops * (step - 1)
    )
    got = axis.exchange(sends, pos, name)
    narrow = wide // axis.digits[pos - 1] if pos else wide
    if pos == 0 or (side == 1 and narrow % LANES):

        def last(left_ref, right_ref, *refs):
            refs[-1][...] = add_up([block(left_ref, right_ref, 0)] + [r[...] for r in refs[:-1]])

        total = run(name + "_rest", last, [(shape, F32)], [left, right, *got], flops=flops)[0]
        if pos == 0:
            return [total]
        parts = [
            lax.slice_in_dim(total, k * narrow, (k + 1) * narrow, axis=side)
            for k in range(axis.digits[pos - 1])
        ]
    else:
        count = axis.digits[pos - 1]

        def last(left_ref, right_ref, *refs):
            outs = refs[-count:]
            total = add_up([block(left_ref, right_ref, 0)] + [r[...] for r in refs[:-count]])
            for k, out in enumerate(outs):
                at = slice(k * narrow, (k + 1) * narrow)
                out[...] = (total[at, :] if side == 0 else total[:, at]).astype(out.dtype)

        small = (narrow, shape[1]) if side == 0 else (shape[0], narrow)
        outs = [(small, F32)] + [(small, BF)] * (count - 1)
        parts = run(name + "_rest", last, outs, [left, right, *got], flops=flops)
    return axis.scatter(parts[0], [p.astype(BF) for p in parts[1:]], side, name, pos - 1)


def make_per_device(mesh):
    dp = Axis("dp", mesh.shape["dp"], 4)
    tp = Axis("tensor", mesh.shape["tensor"], 2)
    outer = tp.digits[-1]
    last = len(tp.digits) - 1

    def per_device(
        resid_in,
        segment_ids,
        out_grad,
        norm1_gain,
        norm1_shift,
        qkv_weight,
        qv_bias,
        proj_weight,
        proj_bias,
        norm2_gain,
        norm2_shift,
        up_weight,
        up_bias,
        down_weight,
        down_bias,
    ):
        rows_dev, width = resid_in.shape
        row = lambda v: v.reshape(1, -1)
        cols = Columns(dp.order(), width)

        normed_one, cot, g_down_bias = entry(
            cols, resid_in, out_grad, row(norm1_gain), row(norm1_shift)
        )
        qkv_full = dp.gather(qkv_weight, 1, "w_qkv")
        rows_one = tp.gather(normed_one, 0, "rows_one")
        proj_full = dp.gather(proj_weight, 1, "w_proj")
        up_full = dp.gather(up_weight, 0, "w_up")
        down_full = dp.gather(down_weight, 1, "w_down")
        cot_all = tp.gather(cot, 0, "cot")

        t_order = tp.order()
        positions = (t_order[:, None] * rows_dev + jnp.arange(rows_dev)[None]).reshape(-1)
        seg = jnp.concatenate(
            [
                lax.dynamic_slice_in_dim(segment_ids[0], t_order[k] * rows_dev, rows_dev)
                for k in range(tp.size)
            ]
        )
        place = (row(seg), row(positions), seg[:, None], positions[:, None])

        saved, keep, sends = attention(rows_one, qkv_full, qv_bias, place, proj_full, outer)
        attn_parts = tp.scatter(keep, sends, 0, "attn", last)
        middle, normed_two = second_norm(
            cols, resid_in, attn_parts, row(proj_bias), row(norm2_gain), row(norm2_shift)
        )
        rows_two = tp.gather(normed_two, 0, "rows_two")
        hidden, slope = feed_up(rows_two, up_full, row(up_bias))
        down_parts = weight_grad("g_down", dp, hidden, cot_all, 1)
        d_upper, g_upbias, keep, sends = feed_back(cot_all, down_full, slope, up_full, outer)
        two_parts = tp.scatter(keep, sends, 0, "d_two", last)
        up_parts = weight_grad("g_up", dp, rows_two, d_upper, 0)
        keep, sends = feed_down(hidden, down_full, outer)
        mlp_parts = tp.scatter(keep, sends, 0, "mlp", last)
        resid_out = last_add(cols, middle, mlp_parts, row(down_bias))
        d_middle, g_gain_two, g_shift_two, d_middle_b, g_proj_bias = norm_back(
            "norm_back_two", cols, middle, two_parts, row(norm2_gain), out_grad, True
        )
        middle_all = tp.gather(cols.relative(d_middle_b), 0, "d_middle")
        dqkv, g_qvbias, keep, sends = attention_back(
            middle_all, proj_full, saved, place, qkv_full, outer
        )
        one_parts = tp.scatter(keep, sends, 0, "d_one", last)
        qkv_parts = weight_grad("g_qkv", dp, rows_one, dqkv, 0)
        proj_parts = weight_grad("g_proj", dp, saved[3], middle_all, 1)
        resid_grad, g_gain_one, g_shift_one = norm_back(
            "norm_back_one", cols, resid_in, one_parts, row(norm1_gain), d_middle, False
        )
        sums = jnp.concatenate(
            [g_gain_one, g_shift_one, g_proj_bias, g_gain_two, g_shift_two, g_down_bias], axis=0
        )
        sums = tp.total(sums, "sum_t")
        packed = jnp.concatenate([sums.reshape(-1), g_qvbias.reshape(-1), g_upbias.reshape(-1)])
        packed = dp.total(packed, "sum_d")
        cut = sums.size
        vec = packed[:cut].reshape(sums.shape)
        qv_bias_grad = packed[cut : cut + g_qvbias.size].reshape(g_qvbias.shape)
        up_bias_grad = packed[cut + g_qvbias.size :]
        down_grad, up_grad, proj_grad = (add_up(p) for p in (down_parts, up_parts, proj_parts))
        flat = add_up(qkv_parts)
        qkv_grad = jnp.stack(jnp.split(flat, 3, axis=1))
        return (
            resid_out,
            resid_grad,
            vec[0],
            vec[1],
            qkv_grad,
            qv_bias_grad,
            proj_grad,
            vec[2],
            vec[3],
            vec[4],
            up_grad,
            up_bias_grad,
            down_grad,
            vec[5],
        )

    return per_device


def solution(mesh):
    rows = P(("dp", "tensor"), None)
    qkv = P(None, "dp", "tensor")
    in_specs = (
        rows,
        P("dp", None),
        rows,
        P(),
        P(),
        qkv,
        P(None, "tensor"),
        P("tensor", "dp"),
        P(),
        P(),
        P(),
        P("dp", "tensor"),
        P("tensor"),
        P("tensor", "dp"),
        P(),
    )
    out_specs = (
        rows,
        rows,
        P(),
        P(),
        qkv,
        P(None, "tensor"),
        P("tensor", "dp"),
        P(),
        P(),
        P(),
        P("dp", "tensor"),
        P("tensor"),
        P("tensor", "dp"),
        P(),
    )
    return jax.shard_map(
        make_per_device(mesh), mesh=mesh, in_specs=in_specs, out_specs=out_specs, check_vma=False
    )
```
